512 devices in a mesh: row: 16 (over y, core), col: 32 (over z, x).
Axes of the slice: x: 4, y: 8, z: 8, core: 2. Of those that a mesh axis runs over, the one named last changes fastest.
Arguments:
- src_embed: bfloat16 [64, 32768], P('col', 'row'), may hold values from -1.5 to 1.5
- src_left: bfloat16 [64, 32768], P('col', 'row'), may hold values from -0.75 to 0.75
- src_right: bfloat16 [64, 32768], P('col', 'row'), may hold values from -4.5 to 4.5, as said below
- src_logit: float32 [32768], P('row'), may hold values from -2 to 3.2
- src_weight: float32 [32768], P('row'), may hold values from 1 to 10
- tgt_embed: bfloat16 [64, 65536], P('row', 'col'), may hold values from -1.5 to 1.5
- tgt_left: bfloat16 [64, 65536], P('row', 'col'), may hold values from -0.75 to 0.75
- tgt_right: bfloat16 [64, 65536], P('row', 'col'), may hold values from -4.5 to 4.5, as said below
- tgt_logit: float32 [65536], P('col'), may hold values from -2 to 3.2
- tgt_weight: float32 [65536], P('col'), may hold values from 1 to 10
Outputs:
- row_potential: float32 [32768], P('row')
- col_potential: float32 [65536], P('col')
- new_core: float32 [64, 64], replicated
The draws below stay inside these ranges and needn't reach their ends.
Inputs may be any that keep to these rules, and one draw needn't show every extreme that they name: `src_right`: each rank's row sums to about zero over the points. `tgt_right`: each rank's row sums to about zero over the points.
All inputs are finite; a program needn't handle non-finite values.
Results may differ from the reference program's by a relative error of at most 0.012.
Values may be sent and summed in bfloat16 or wider, within the bound.
No kernel may reach another device: no remote copies, remote signals or barrier semaphores. Data moves between devices by JAX's collectives and lax.ppermute only.
A program may use at most 64 MiB of HBM per device.

```python
import math
import jax
import jax.numpy as jnp
from jax import lax

R = 64
RD = 2048
SWEEPS = 3
N = 32768
M = 65536


def draw_src_logit(key, part):
    ramp = jnp.arange(N, dtype=jnp.float32) / N
    noise = jnp.clip(jax.random.normal(key, (N,), jnp.float32), -4.0, 4.0)
    return 1.1 * ramp + 0.5 * noise


def draw_tgt_logit(key, part):
    ramp = jnp.arange(M, dtype=jnp.float32) / M
    noise = jnp.clip(jax.random.normal(jax.random.fold_in(key, 7), (M,), jnp.float32), -4.0, 4.0)
    return 1.1 * ramp + 0.5 * noise


def centred_factor(key, count):
    values = jnp.clip(jax.random.normal(key, (R, count), jnp.float32), -4.0, 4.0)
    values = values - jnp.mean(values, axis=1, keepdims=True)
    return values.astype(jnp.bfloat16)


def draw_src_right(key, part):
    return centred_factor(jax.random.fold_in(key, 11), N)


def draw_tgt_right(key, part):
    return centred_factor(jax.random.fold_in(key, 13), M)


def block_scale(stream_key, dims, split, low, high):
    loudness, own = 1.0, jax.random.fold_in(stream_key, 6)
    for dim, parts in split:
        heights = jnp.exp(jax.random.uniform(jax.random.fold_in(own, dim), (parts,), jnp.float32, low / len(split), high / len(split)))
        loudness = loudness * jnp.repeat(heights, dims[dim] // parts).reshape([-1 if axis == dim else 1 for axis in range(len(dims))])
    return loudness


def normal_values(own_key, dims, spread, bound, cuts=(), kind=jnp.bfloat16):
    result = jax.random.normal(own_key, dims, jnp.float32) * spread
    if len(cuts) > 0:
        result = block_scale(own_key, dims, cuts, -0.22, 0.18) * result
    return jnp.clip(result, min=-bound, max=bound).astype(kind)


def setup_inputs(seed: int = 0) -> dict:
    splits = jax.random.split(jax.random.key(seed), 11)
    return {
        "src_embed": jnp.clip(jax.random.uniform(splits[0], (R, N), jnp.float32, -1.5, 1.5) * block_scale(splits[0], (R, N), ((0, 32), (1, 16)), -0.4, 0.0), -1.5, 1.5).astype(jnp.bfloat16),
        "src_left": normal_values(splits[1], (R, N), R ** -0.5, 0.75, ((0, 32), (1, 16))),
        "src_right": draw_src_right(jax.random.fold_in(splits[10], 71), 0),
        "src_logit": draw_src_logit(jax.random.fold_in(splits[10], 71), 0),
        "src_weight": jnp.clip(jnp.exp(math.log(10.0) - 2.3025851 * jax.random.uniform(splits[4], (N,), jnp.float32) ** block_scale(splits[4], (N,), ((0, 16),), -0.2, 0.2)), 1.0, 10.0),
        "tgt_embed": jnp.clip(jax.random.uniform(splits[5], (R, M), jnp.float32, -1.5, 1.5) * block_scale(splits[5], (R, M), ((0, 16), (1, 32)), -0.4, 0.0), -1.5, 1.5).astype(jnp.bfloat16),
        "tgt_left": normal_values(splits[6], (R, M), R ** -0.5, 0.75, ((0, 16), (1, 32))),
        "tgt_right": draw_tgt_right(jax.random.fold_in(splits[10], 71), 0),
        "tgt_logit": draw_tgt_logit(jax.random.fold_in(splits[10], 71), 0),
        "tgt_weight": jnp.clip(jnp.exp(math.log(10.0) - 2.3025851 * jax.random.uniform(splits[9], (M,), jnp.float32) ** block_scale(splits[9], (M,), ((0, 32),), -0.2, 0.2)), 1.0, 10.0),
    }


def inner_dot(left_side, right_side):
    return lax.dot_general(left_side, right_side, (((0,), (0,)), ((), ())), preferred_element_type=jnp.float32)

def reference(src_embed, src_left, src_right, src_logit, src_weight, tgt_embed, tgt_left, tgt_right, tgt_logit, tgt_weight):
    highest = lax.Precision.HIGHEST
    block_count = N // RD
    embed_scaled = src_embed * 0.125

    def opening(position):
        start_row = (position * RD).astype(jnp.int32)
        embed_rows = lax.dynamic_slice_in_dim(embed_scaled, start_row, RD, 1)
        logit_rows = lax.dynamic_slice_in_dim(src_logit, start_row, RD, 0)
        start_tile = jnp.exp(logit_rows[:, None] + tgt_logit[None, :] + inner_dot(embed_rows, tgt_embed)).astype(jnp.bfloat16)
        tile_total = jnp.sum(start_tile, dtype=jnp.float32)
        side_rows = lax.dot_general(start_tile, tgt_right, (((1,), (1,)), ((), ())), preferred_element_type=jnp.float32)
        return (tile_total, side_rows)
    tile_totals, side_rows = lax.map(opening, jnp.arange(block_count, dtype=jnp.int32))
    side_sum = side_rows.reshape(N, R)
    grand_total = jnp.sum(tile_totals)
    mass_scale = math.sqrt(N * M)
    mixing = mass_scale * jnp.dot(src_right.astype(jnp.float32), side_sum, precision=highest) / grand_total
    row_factor = (2.0 * jnp.dot(mixing.T, src_left.astype(jnp.float32), precision=highest)).astype(jnp.bfloat16)
    left_stack = jnp.concatenate([embed_scaled, row_factor], axis=0)
    right_stack = jnp.concatenate([tgt_embed, tgt_left], axis=0)
    log_shift = -jnp.log(grand_total)

    def kernel_rows(position):
        start_row = (position * RD).astype(jnp.int32)
        left_rows = lax.dynamic_slice_in_dim(left_stack, start_row, RD, 1)
        logit_rows = lax.dynamic_slice_in_dim(src_logit, start_row, RD, 0)
        return jnp.exp(logit_rows[:, None] + tgt_logit[None, :] + log_shift + inner_dot(left_rows, right_stack)).astype(jnp.bfloat16)
    kernel = lax.map(kernel_rows, jnp.arange(block_count, dtype=jnp.int32)).reshape(N, M)
    row_mass = src_weight / jnp.sum(src_weight)
    col_mass = tgt_weight / jnp.sum(tgt_weight)
    col_scale = jnp.ones((M,), jnp.float32)
    row_scale = jnp.ones((N,), jnp.float32)
    for sweep in range(SWEEPS):
        row_total = jnp.dot(kernel, col_scale.astype(jnp.bfloat16), preferred_element_type=jnp.float32)
        row_scale = row_mass / row_total
        col_total = lax.dot_general(kernel, row_scale.astype(jnp.bfloat16), (((0,), (0,)), ((), ())), preferred_element_type=jnp.float32)
        col_scale = col_mass / col_total
    scaled_right = (tgt_right * col_scale[None, :]).astype(jnp.bfloat16)
    closing_side = lax.dot_general(kernel, scaled_right, (((1,), (1,)), ((), ())), preferred_element_type=jnp.float32)
    closing_side = row_scale[:, None] * closing_side
    new_core = mass_scale * jnp.dot(src_right.astype(jnp.float32), closing_side, precision=highest)
    row_potential = jnp.log(row_scale) + math.log(N) + math.log(M)
    col_potential = jnp.log(col_scale)
    return (row_potential, col_potential, new_core)
```

```python
import math

import jax
import jax.numpy as jnp
from jax import lax
from jax.sharding import Mesh
from jax.sharding import PartitionSpec as P

SWEEPS = 3
ROW = ("row_0", "row_1")
COL = ("col_0", "col_1")


def in_one_piece(arrays, axis, dim, along):
    ends, at = ([], 0)
    for a in arrays[:-1]:
        at += a.shape[along]
        ends.append(at)
    both = jnp.concatenate(arrays, axis=along)
    return tuple(jnp.split(lax.all_gather(both, axis, axis=dim, tiled=True), ends, axis=along))


def sent_to_all(value, axis):
    peers = lax.axis_size(axis)
    return lax.all_to_all(
        jnp.broadcast_to(value[None], (peers, *value.shape)), axis, 0, 0, tiled=True
    )


def taken_together(value, axis):
    received = sent_to_all(value.astype(jnp.bfloat16), axis)
    return received.astype(jnp.float32).sum(axis=0)


def core_over_all(core):
    flat = core.reshape(-1, 128)
    return taken_together(taken_together(flat, ROW), COL).reshape(core.shape)


def inner_dot(left_side, right_side):
    return lax.dot_general(
        left_side, right_side, (((0,), (0,)), ((), ())), preferred_element_type=jnp.float32
    )


def body(
    src_embed,
    src_left,
    src_right,
    src_logit,
    src_weight,
    tgt_embed,
    tgt_left,
    tgt_right,
    tgt_logit,
    tgt_weight,
):
    highest = lax.Precision.HIGHEST
    row_count = src_logit.shape[0]
    col_count = tgt_logit.shape[0]
    n_all = row_count * lax.axis_size(ROW)
    m_all = col_count * lax.axis_size(COL)
    src_mine = jnp.concatenate((src_embed, src_left, src_right), axis=1)
    src_full = sent_to_all(src_mine, COL).reshape(-1, src_mine.shape[1])
    embed_full, left_full, right_full = jnp.split(src_full, 3, axis=1)
    tgt_embed_full, tgt_left_full, tgt_right_full = in_one_piece(
        (tgt_embed, tgt_left, tgt_right), ROW, 0, 1
    )
    rank_width = tgt_embed_full.shape[0]
    embed_scaled = embed_full * 0.125
    block_rows = 512
    block_count = row_count // block_rows
    positions = jnp.arange(block_count, dtype=jnp.int32)

    def opening(position):
        start_row = position * block_rows
        embed_rows = lax.dynamic_slice_in_dim(embed_scaled, start_row, block_rows, 1)
        logit_rows = lax.dynamic_slice_in_dim(src_logit, start_row, block_rows, 0)
        start_tile = jnp.exp(
            logit_rows[:, None] + tgt_logit[None, :] + inner_dot(embed_rows, tgt_embed_full)
        ).astype(jnp.bfloat16)
        tile_total = jnp.sum(start_tile, dtype=jnp.float32)
        side_rows = lax.dot_general(
            start_tile, tgt_right_full, (((1,), (1,)), ((), ())), preferred_element_type=jnp.float32
        )
        return (tile_total, side_rows)

    tile_totals, side_rows = lax.map(opening, positions)
    side_sum = side_rows.reshape(row_count, rank_width)
    local_total = jnp.sum(tile_totals)
    core_part = jnp.dot(right_full.astype(jnp.float32), side_sum, precision=highest)
    row_sums = sent_to_all(jnp.stack([local_total, jnp.sum(src_weight)]), ROW).sum(axis=0)
    col_sums = sent_to_all(jnp.stack([row_sums[0], jnp.sum(tgt_weight)]), COL).sum(axis=0)
    grand_total, src_mass, tgt_mass = col_sums[0], row_sums[1], col_sums[1]
    core_sum = core_over_all(core_part)
    mass_scale = math.sqrt(n_all * m_all)
    mixing = mass_scale * core_sum / grand_total
    row_factor = (2.0 * jnp.dot(mixing.T, left_full.astype(jnp.float32), precision=highest)).astype(
        jnp.bfloat16
    )
    left_stack = jnp.concatenate([embed_scaled, row_factor], axis=0)
    right_stack = jnp.concatenate([tgt_embed_full, tgt_left_full], axis=0)
    log_shift = -jnp.log(grand_total)

    def kernel_rows(position):
        start_row = position * block_rows
        left_rows = lax.dynamic_slice_in_dim(left_stack, start_row, block_rows, 1)
        logit_rows = lax.dynamic_slice_in_dim(src_logit, start_row, block_rows, 0)
        return jnp.exp(
            logit_rows[:, None] + tgt_logit[None, :] + log_shift + inner_dot(left_rows, right_stack)
        ).astype(jnp.bfloat16)

    kernel_tile = lax.map(kernel_rows, positions).reshape(row_count, col_count)
    row_mass = src_weight / src_mass
    col_mass = tgt_weight / tgt_mass
    col_scale = jnp.ones((col_count,), jnp.float32)
    row_scale = jnp.ones((row_count,), jnp.float32)
    for sweep in range(SWEEPS):
        row_total = taken_together(
            jnp.dot(
                kernel_tile, col_scale.astype(jnp.bfloat16), preferred_element_type=jnp.float32
            ),
            COL,
        )
        row_scale = row_mass / row_total
        col_total = taken_together(
            lax.dot_general(
                kernel_tile,
                row_scale.astype(jnp.bfloat16),
                (((0,), (0,)), ((), ())),
                preferred_element_type=jnp.float32,
            ),
            ROW,
        )
        col_scale = col_mass / col_total
    scaled_right = (tgt_right_full * col_scale[None, :]).astype(jnp.bfloat16)
    closing_side = row_scale[:, None] * lax.dot_general(
        kernel_tile, scaled_right, (((1,), (1,)), ((), ())), preferred_element_type=jnp.float32
    )
    core_local = jnp.dot(right_full.astype(jnp.float32), closing_side, precision=highest)
    new_core = mass_scale * core_over_all(core_local)
    row_potential = jnp.log(row_scale) + math.log(n_all) + math.log(m_all)
    col_potential = jnp.log(col_scale)
    return (row_potential, col_potential, new_core)


def solution(mesh):
    torus = Mesh(mesh.devices.reshape(8, 2, 8, 4), ("row_0", "row_1", "col_0", "col_1"))
    placed = (
        P(COL, ROW),
        P(COL, ROW),
        P(COL, ROW),
        P(ROW),
        P(ROW),
        P(ROW, COL),
        P(ROW, COL),
        P(ROW, COL),
        P(COL),
        P(COL),
    )
    return jax.shard_map(
        body, mesh=torus, in_specs=placed, out_specs=(P(ROW), P(COL), P()), check_vma=False
    )
```

```python
import functools
import math

import jax
import jax.numpy as jnp
from jax import lax
from jax.experimental import pallas as pl
from jax.experimental.pallas import tpu as pltpu
from jax.sharding import Mesh
from jax.sharding import PartitionSpec as P

SWEEPS = 3
ROW = ("row_0", "row_1")
COL = ("col_0", "col_1")
F32 = jnp.float32
BF16 = jnp.bfloat16
LANES = 128
BLOCK = 256
PAD = 16

VMEM = pl.BlockSpec(memory_space=pltpu.VMEM)
CONTRACT_FIRST = (((0,), (0,)), ((), ()))
CONTRACT_LAST = (((1,), (1,)), ((), ()))
PLAIN = (((1,), (0,)), ((), ()))


def dot(a, b, dims):
    return lax.dot_general(a, b, dims, preferred_element_type=F32)


def three_parts(v):
    high = v.astype(BF16).astype(F32)
    rest = v - high
    mid = rest.astype(BF16).astype(F32)
    low = (rest - mid).astype(BF16).astype(F32)
    return high, mid, low


def logit_rows(v, first):
    n = v.shape[1]
    row = lax.broadcasted_iota(jnp.int32, (PAD, n), 0)
    at, ones = (0, 3) if first else (3, 0)
    out = jnp.where((row >= ones) & (row < ones + 3), 1.0, 0.0)
    for index, part in enumerate(three_parts(v)):
        out = jnp.where(row == at + index, jnp.broadcast_to(part, (PAD, n)), out)
    return out.astype(BF16)


def to_lanes(v, flat_ref):
    for s in range(v.shape[0]):
        flat_ref[:, s * LANES : (s + 1) * LANES] = jnp.broadcast_to(v[s : s + 1], (8, LANES))
    return flat_ref[...]


def to_tiles(row, tile_ref):
    for s in range(tile_ref.shape[0]):
        tile_ref[s : s + 1, :] = row[:, s * LANES : (s + 1) * LANES]
    return tile_ref[...]


def send(out_ref, v):
    v = v.astype(out_ref.dtype)
    for p in range(out_ref.shape[0]):
        out_ref[p] = v


def received(ref):
    total = ref[0].astype(F32)
    for p in range(1, ref.shape[0]):
        total = total + ref[p].astype(F32)
    return total


def halves_on_lanes(core, rank):
    half = rank // 2
    lane = lax.broadcasted_iota(jnp.int32, (half, 2 * rank), 1)
    return jnp.where(lane < rank, core[:half], core[half:rank])


def opening_kernel(src, tgt, src_logit, tgt_logit, src_weight, tgt_weight, out, xs, xt, right, acc):
    rank = src.shape[0]
    n = src_logit.shape[1]
    m = tgt_logit.shape[1]
    xs[:rank] = (src[:, :n].astype(F32) * 0.125).astype(BF16)
    xs[rank:] = logit_rows(src_logit[...], True)
    xt[:rank] = tgt[:, :m]
    xt[rank:] = logit_rows(tgt_logit[...], False)
    right[:rank] = tgt[:, 2 * m :]
    right[rank : 2 * rank] = tgt[:, 2 * m :]
    row = lax.broadcasted_iota(jnp.int32, (PAD, m), 0)
    right[2 * rank :] = jnp.where(row == 0, 1.0, 0.0).astype(BF16)
    acc[...] = jnp.zeros_like(acc)
    one_row = jnp.where(
        lax.broadcasted_iota(jnp.int32, (PAD, BLOCK), 0) == 0, 1.0, 0.0
    ).astype(BF16)

    def step(b, carry):
        at = pl.multiple_of(b * BLOCK, BLOCK)
        x = dot(xs[:, pl.ds(at, BLOCK)], xt[...], CONTRACT_FIRST)
        tile = jnp.exp(x).astype(BF16)
        side = dot(tile, right[...], CONTRACT_LAST)
        left = jnp.concatenate([src[:, pl.ds(2 * n + at, BLOCK)], one_row], axis=0)
        for part in three_parts(side):
            acc[...] += dot(left, part.astype(BF16), PLAIN)
        return carry

    lax.fori_loop(0, n // BLOCK, step, 0)
    core = halves_on_lanes(acc[:, : 2 * rank], rank)
    total = acc[rank : rank + 1, 2 * rank : 2 * rank + 1]
    src_sum = jnp.sum(src_weight[...], keepdims=True)
    tgt_sum = jnp.sum(tgt_weight[...], keepdims=True)
    lane = lax.broadcasted_iota(jnp.int32, (8, LANES), 1)
    sums = jnp.where(lane == 0, total, jnp.where(lane == 1, src_sum, jnp.where(lane == 2, tgt_sum, 0.0)))
    send(out, jnp.concatenate([core, sums], axis=0))


def relay_kernel(y, out):
    send(out, received(y))


def tile_kernel(
    mass_scale, row_peers, col_peers,
    z, src, tgt, src_logit, tgt_logit, src_weight, tgt_weight,
    kernel, out, row_mass, col_mass, xs, xt, totals, tiles,
):
    rank = src.shape[0]
    half = rank // 2
    n = src_logit.shape[1]
    m = tgt_logit.shape[1]
    sums = received(z)
    grand_total = sums[half : half + 1, 0:1]
    row_mass[...] = src_weight[...] / (sums[half : half + 1, 1:2] / col_peers)
    col_mass[...] = tgt_weight[...] / (sums[half : half + 1, 2:3] / row_peers)
    mixing = mass_scale * sums[:half] / grand_total
    parts = jnp.concatenate(three_parts(mixing), axis=0).astype(BF16)
    top = src[:half, n : 2 * n]
    bottom = src[half:, n : 2 * n]
    top = dot(parts, jnp.concatenate([top, top, top], axis=0), CONTRACT_FIRST)
    bottom = dot(parts, jnp.concatenate([bottom, bottom, bottom], axis=0), CONTRACT_FIRST)
    xs[:rank] = (src[:, :n].astype(F32) * 0.125).astype(BF16)
    xs[rank : 2 * rank] = (2.0 * (top[:rank] + bottom[rank:])).astype(BF16)
    xs[2 * rank :] = logit_rows(src_logit[...], True)
    xt[:rank] = tgt[:, :m]
    xt[rank : 2 * rank] = tgt[:, m : 2 * m]
    xt[2 * rank :] = logit_rows(tgt_logit[...] - jnp.log(grand_total), False)
    ones = jnp.ones((PAD, m), BF16)

    def step(b, carry):
        at = pl.multiple_of(b * BLOCK, BLOCK)
        x = dot(xs[:, pl.ds(at, BLOCK)], xt[...], CONTRACT_FIRST)
        tile = jnp.exp(x).astype(BF16)
        kernel[pl.ds(at, BLOCK), :] = tile
        totals[:, pl.ds(at, BLOCK)] = dot(ones, tile, CONTRACT_LAST)[:8]
        return carry

    lax.fori_loop(0, n // BLOCK, step, 0)
    send(out, to_tiles(totals[0:1, :], tiles))


def sweep_kernel(over_rows, y, mass, kernel, scale, out, flat, tiles):
    s = mass[...] / received(y)
    scale[...] = s
    weights = to_lanes(s, flat).astype(BF16)
    total = dot(weights, kernel[...], PLAIN if over_rows else CONTRACT_LAST)
    send(out, to_tiles(total[0:1], tiles))


def closing_kernel(
    shift, y, mass, row_scale, kernel, src, tgt, row_potential, col_potential, out, flat, twice, closing
):
    rank = src.shape[0]
    n, m = kernel.shape
    col_scale = mass[...] / received(y)
    col_potential[...] = jnp.log(col_scale)
    row_potential[...] = jnp.log(row_scale[...]) + shift
    cols = to_lanes(col_scale, flat)
    scaled = (tgt[:, 2 * m :].astype(F32) * cols[0:1]).astype(BF16)
    twice[:rank] = scaled
    twice[rank:] = scaled
    closing[...] = dot(kernel[...], twice[...], CONTRACT_LAST)
    rows = to_lanes(row_scale[...], flat)
    left = src[:, 2 * n :].astype(F32) * rows[0:1]
    core = lax.dot_general(
        left, closing[...], PLAIN, precision=lax.Precision.HIGHEST, preferred_element_type=F32
    )
    send(out, halves_on_lanes(core, rank))


def final_kernel(mass_scale, y, out):
    out[...] = mass_scale * received(y)


def call(body, outs, scratch, *args):
    return pl.pallas_call(
        body,
        out_shape=[jax.ShapeDtypeStruct(s, d) for s, d in outs],
        in_specs=[VMEM] * len(args),
        out_specs=[VMEM] * len(outs),
        scratch_shapes=[pltpu.VMEM(s, d) for s, d in scratch],
        compiler_params=pltpu.CompilerParams(vmem_limit_bytes=24 << 20),
    )(*args)


def exchange(value, axis):
    return lax.all_to_all(value, axis, 0, 0, tiled=True)


def body(
    src_embed,
    src_left,
    src_right,
    src_logit,
    src_weight,
    tgt_embed,
    tgt_left,
    tgt_right,
    tgt_logit,
    tgt_weight,
):
    n, m = src_logit.shape[0], tgt_logit.shape[0]
    row_peers, col_peers = lax.axis_size(ROW), lax.axis_size(COL)
    n_all, m_all = n * row_peers, m * col_peers
    rank = src_embed.shape[0] * col_peers
    half = rank // 2
    mass_scale = math.sqrt(n_all * m_all)
    nt, mt = n // LANES, m // LANES

    mine = jnp.concatenate((src_embed, src_left, src_right), axis=1)
    src = exchange(jnp.broadcast_to(mine[None], (col_peers, *mine.shape)), COL).reshape(rank, 3 * n)
    mine = jnp.concatenate((tgt_embed, tgt_left, tgt_right), axis=1)
    tgt = lax.all_gather(mine, ROW, axis=0, tiled=True)
    src_logit, tgt_logit = src_logit.reshape(1, n), tgt_logit.reshape(1, m)
    src_weight, tgt_weight = src_weight.reshape(nt, LANES), tgt_weight.reshape(mt, LANES)

    (part,) = call(
        opening_kernel,
        [((row_peers, half + 8, LANES), F32)],
        [
            ((rank + PAD, n), BF16),
            ((rank + PAD, m), BF16),
            ((2 * rank + PAD, m), BF16),
            ((rank + PAD, 2 * rank + PAD), F32),
        ],
        src, tgt, src_logit, tgt_logit, src_weight, tgt_weight,
    )
    (part,) = call(relay_kernel, [((col_peers, half + 8, LANES), F32)], [], exchange(part, ROW))
    kernel, part, row_mass, col_mass = call(
        functools.partial(tile_kernel, mass_scale, row_peers, col_peers),
        [
            ((n, m), BF16),
            ((col_peers, nt, LANES), BF16),
            ((nt, LANES), F32),
            ((mt, LANES), F32),
        ],
        [
            ((2 * rank + PAD, n), BF16),
            ((2 * rank + PAD, m), BF16),
            ((8, n), F32),
            ((nt, LANES), F32),
        ],
        exchange(part, COL), src, tgt, src_logit, tgt_logit, src_weight, tgt_weight,
    )
    for sweep in range(SWEEPS):
        row_scale, part = call(
            functools.partial(sweep_kernel, True),
            [((nt, LANES), F32), ((row_peers, mt, LANES), BF16)],
            [((8, n), F32), ((mt, LANES), F32)],
            exchange(part, COL), row_mass, kernel,
        )
        part = exchange(part, ROW)
        if sweep + 1 < SWEEPS:
            _, part = call(
                functools.partial(sweep_kernel, False),
                [((mt, LANES), F32), ((col_peers, nt, LANES), BF16)],
                [((8, m), F32), ((nt, LANES), F32)],
                part, col_mass, kernel,
            )
    row_potential, col_potential, part = call(
        functools.partial(closing_kernel, math.log(n_all) + math.log(m_all)),
        [((nt, LANES), F32), ((mt, LANES), F32), ((row_peers, half, LANES), BF16)],
        [((8, max(n, m)), F32), ((2 * rank, m), BF16), ((n, 2 * rank), F32)],
        part, col_mass, row_scale, kernel, src, tgt,
    )
    (part,) = call(relay_kernel, [((col_peers, half, LANES), BF16)], [], exchange(part, ROW))
    (core,) = call(
        functools.partial(final_kernel, mass_scale), [((half, LANES), F32)], [], exchange(part, COL)
    )
    new_core = jnp.concatenate([core[:, :rank], core[:, rank:]], axis=0)
    return (row_potential.reshape(n), col_potential.reshape(m), new_core)


def solution(mesh):
    torus = Mesh(mesh.devices.reshape(8, 2, 8, 4), ("row_0", "row_1", "col_0", "col_1"))
    placed = (
        P(COL, ROW),
        P(COL, ROW),
        P(COL, ROW),
        P(ROW),
        P(ROW),
        P(ROW, COL),
        P(ROW, COL),
        P(ROW, COL),
        P(COL),
        P(COL),
    )
    return jax.shard_map(
        body, mesh=torus, in_specs=placed, out_specs=(P(ROW), P(COL), P()), check_vma=False
    )
```

```python
import functools
import math

import jax
import jax.numpy as jnp
from jax import lax
from jax.experimental import pallas as pl
from jax.experimental.pallas import tpu as pltpu
from jax.sharding import Mesh
from jax.sharding import PartitionSpec as P

SWEEPS = 3
ROW = ("row_0", "row_1")
COL = ("col_0", "col_1")
F32 = jnp.float32
BF16 = jnp.bfloat16
LANES = 128
CHUNK = 4
PAD = 16

VMEM = pl.BlockSpec(memory_space=pltpu.VMEM)
FIRST = (((0,), (0,)), ((), ()))
LAST = (((1,), (1,)), ((), ()))
PLAIN = (((1,), (0,)), ((), ()))


def dot(a, b, dims):
    return lax.dot_general(a, b, dims, preferred_element_type=F32)


def three_parts(v):
    high = v.astype(BF16).astype(F32)
    rest = v - high
    mid = rest.astype(BF16).astype(F32)
    low = (rest - mid).astype(BF16).astype(F32)
    return high, mid, low


def logit_rows(v, first):
    n = v.shape[1]
    row = lax.broadcasted_iota(jnp.int32, (PAD, n), 0)
    at, ones = (0, 3) if first else (3, 0)
    out = jnp.where((row >= ones) & (row < ones + 3), 1.0, 0.0)
    for index, part in enumerate(three_parts(v)):
        out = jnp.where(row == at + index, jnp.broadcast_to(part, (PAD, n)), out)
    return out.astype(BF16)


def to_lanes(v, flat_ref):
    for s in range(v.shape[0]):
        flat_ref[:, s * LANES : (s + 1) * LANES] = jnp.broadcast_to(v[s : s + 1], (8, LANES))
    return flat_ref[...]


def to_tiles(row, tile_ref):
    for s in range(tile_ref.shape[0]):
        tile_ref[s : s + 1, :] = row[:, s * LANES : (s + 1) * LANES]
    return tile_ref[...]


def send(out_ref, v):
    v = v.astype(out_ref.dtype)
    for p in range(out_ref.shape[0]):
        out_ref[p] = v


def received(ref):
    total = ref[0].astype(F32)
    for p in range(1, ref.shape[0]):
        total = total + ref[p].astype(F32)
    return total


def halves_on_lanes(core, rank):
    half = rank // 2
    lane = lax.broadcasted_iota(jnp.int32, (half, 2 * rank), 1)
    return jnp.where(lane < rank, core[:half], core[half:rank])


def fetch(there, here, sem):
    copies = [pltpu.make_async_copy(t, h, sem.at[k]) for k, (t, h) in enumerate(zip(there, here))]
    for copy in copies:
        copy.start()
    return copies


def pack_kernel(*refs):
    there, (src_out, tgt_out), here, sem = refs[:6], refs[6:8], refs[8:14], refs[14]
    for copy in fetch(there, here, sem):
        copy.wait()
    mine = jnp.concatenate([ref[...] for ref in here[:3]], axis=1)
    for p in range(src_out.shape[0]):
        src_out[p] = mine
    tgt_out[...] = jnp.concatenate([ref[...] for ref in here[3:]], axis=1)


def opening_kernel(
    src, tgt, src_logit_in, tgt_logit_in, src_weight_in, tgt_weight_in, out,
    xs, xt, right, src_logit, tgt_logit, src_weight, tgt_weight, sem,
):
    copies = fetch(
        (src_logit_in, tgt_logit_in, src_weight_in, tgt_weight_in),
        (src_logit, tgt_logit, src_weight, tgt_weight),
        sem,
    )
    rank = src.shape[0]
    n = src_logit.shape[1]
    m = tgt_logit.shape[1]
    xs[:rank] = (src[:, :n].astype(F32) * 0.125).astype(BF16)
    xt[:rank] = tgt[:, :m]
    right[:rank] = tgt[:, 2 * m :]
    right[rank : 2 * rank] = tgt[:, 2 * m :]
    row = lax.broadcasted_iota(jnp.int32, (PAD, m), 0)
    right[2 * rank :] = jnp.where(row == 0, 1.0, 0.0).astype(BF16)
    for copy in copies:
        copy.wait()
    xs[rank:] = logit_rows(src_logit[...], True)
    xt[rank:] = logit_rows(tgt_logit[...], False)
    tile = jnp.exp(dot(xs[...], xt[...], FIRST)).astype(BF16)
    side = dot(tile, right[...], LAST)
    row = lax.broadcasted_iota(jnp.int32, (PAD, n), 0)
    left = jnp.concatenate([src[:, 2 * n :], jnp.where(row == 0, 1.0, 0.0).astype(BF16)], axis=0)
    both = sum(dot(left, part.astype(BF16), PLAIN) for part in three_parts(side))
    core = halves_on_lanes(both[:, : 2 * rank], rank)
    total = both[rank : rank + 1, 2 * rank : 2 * rank + 1]
    src_sum = jnp.sum(src_weight[...], keepdims=True)
    tgt_sum = jnp.sum(tgt_weight[...], keepdims=True)
    half = CHUNK // 2
    lane = lax.broadcasted_iota(jnp.int32, (half, LANES), 1)
    sums = jnp.where(
        lane == 0, total, jnp.where(lane == 1, src_sum, jnp.where(lane == 2, tgt_sum, 0.0))
    )
    for p in range(out.shape[0]):
        out[p, :half] = core[p * half : (p + 1) * half]
        out[p, half:] = sums


def relay_kernel(y, out):
    send(out, received(y))


def tile_kernel(
    mass_scale, row_peers, col_peers,
    z, src, tgt, src_logit_in, tgt_logit_in, src_weight_in, tgt_weight_in,
    kernel, out, row_mass, col_mass,
    xs, xt, tiles, core, src_logit, tgt_logit, src_weight, tgt_weight, sem,
):
    copies = fetch(
        (src_logit_in, tgt_logit_in, src_weight_in, tgt_weight_in),
        (src_logit, tgt_logit, src_weight, tgt_weight),
        sem,
    )
    rank = src.shape[0]
    half = rank // 2
    few = CHUNK // 2
    n = src_logit.shape[1]
    m = tgt_logit.shape[1]
    for p in range(row_peers):
        core[p * few : (p + 1) * few] = z[p, :few]
    sums = z[0, few : few + 1]
    grand_total = sums[:, 0:1]
    mixing = mass_scale * core[...] / grand_total
    parts = jnp.concatenate(three_parts(mixing), axis=0).astype(BF16)
    top = src[:half, n : 2 * n]
    bottom = src[half:, n : 2 * n]
    top = dot(parts, jnp.concatenate([top, top, top], axis=0), FIRST)
    bottom = dot(parts, jnp.concatenate([bottom, bottom, bottom], axis=0), FIRST)
    xs[:rank] = (src[:, :n].astype(F32) * 0.125).astype(BF16)
    xs[rank : 2 * rank] = (2.0 * (top[:rank] + bottom[rank:])).astype(BF16)
    for copy in copies:
        copy.wait()
    row_mass[...] = src_weight[...] / (sums[:, 1:2] / col_peers)
    col_mass[...] = tgt_weight[...] / (sums[:, 2:3] / row_peers)
    xs[2 * rank :] = logit_rows(src_logit[...], True)
    xt[:rank] = tgt[:, :m]
    xt[rank : 2 * rank] = tgt[:, m : 2 * m]
    xt[2 * rank :] = logit_rows(tgt_logit[...] - jnp.log(grand_total), False)
    tile = jnp.exp(dot(xs[...], xt[...], FIRST)).astype(BF16)
    kernel[...] = tile
    totals = dot(jnp.ones((PAD, m), BF16), tile, LAST)
    send(out, to_tiles(totals[0:1], tiles))


def sweep_kernel(over_rows, y, mass, kernel, scale, out, flat, tiles):
    s = mass[...] / received(y)
    scale[...] = s
    weights = to_lanes(s, flat).astype(BF16)
    total = dot(weights, kernel[...], PLAIN if over_rows else LAST)
    send(out, to_tiles(total[0:1], tiles))


def side_kernel(shift, row_scale, kernel, src, row_potential, side, flat):
    rank = src.shape[0]
    n = kernel.shape[0]
    row_potential[...] = jnp.log(row_scale[...]) + shift
    rows = to_lanes(row_scale[...], flat)
    left = src[:, 2 * n :].astype(F32) * rows[0:1]
    parts = jnp.concatenate(three_parts(left), axis=0).astype(BF16)
    total = dot(parts, kernel[...], PLAIN)
    side[...] = total[:rank] + total[rank : 2 * rank] + total[2 * rank :]


def closing_kernel(y, mass, side, tgt, col_potential, out, flat, twice):
    rank, m = side.shape
    col_scale = mass[...] / received(y)
    col_potential[...] = jnp.log(col_scale)
    cols = to_lanes(col_scale, flat)
    scaled = (tgt[:, 2 * m :].astype(F32) * cols[0:1]).astype(BF16)
    twice[:rank] = scaled
    twice[rank:] = scaled
    parts = jnp.concatenate(three_parts(side[...]), axis=0).astype(BF16)
    total = dot(parts, twice[...], LAST)
    send(out, halves_on_lanes(total[:rank] + total[rank : 2 * rank] + total[2 * rank :], rank))


def final_kernel(mass_scale, y, out):
    core = mass_scale * received(y)
    half, rank = core.shape[0], core.shape[1] // 2
    out[:half] = core[:, :rank]
    out[half:] = core[:, rank:]


def call(body, outs, scratch, *args, stay=0, room=8):
    here, there = args[: len(args) - stay], args[len(args) - stay :]
    there = [pltpu.with_memory_space_constraint(a, pltpu.HBM) for a in there]
    return pl.pallas_call(
        body,
        out_shape=[jax.ShapeDtypeStruct(s, d) for s, d in outs],
        in_specs=[VMEM] * (len(args) - stay) + [pl.BlockSpec(memory_space=pltpu.HBM)] * stay,
        out_specs=[VMEM] * len(outs),
        scratch_shapes=[pltpu.VMEM(*x) if isinstance(x, tuple) else x for x in scratch],
        compiler_params=pltpu.CompilerParams(vmem_limit_bytes=room << 20),
    )(*here, *there)


def exchange(value, axis):
    return lax.all_to_all(value, axis, 0, 0, tiled=True)


def body(
    src_embed,
    src_left,
    src_right,
    src_logit,
    src_weight,
    tgt_embed,
    tgt_left,
    tgt_right,
    tgt_logit,
    tgt_weight,
):
    n, m = src_logit.shape[0], tgt_logit.shape[0]
    row_peers, col_peers = lax.axis_size(ROW), lax.axis_size(COL)
    n_all, m_all = n * row_peers, m * col_peers
    rank = src_embed.shape[0] * col_peers
    half = rank // 2
    mass_scale = math.sqrt(n_all * m_all)
    nt, mt = n // LANES, m // LANES

    src, tgt = call(
        pack_kernel,
        [
            ((col_peers, rank // col_peers, 3 * n), BF16),
            ((rank // row_peers, 3 * m), BF16),
        ],
        [
            *[(a.shape, BF16) for a in (src_embed, src_left, src_right)],
            *[(a.shape, BF16) for a in (tgt_embed, tgt_left, tgt_right)],
            pltpu.SemaphoreType.DMA((6,)),
        ],
        src_embed, src_left, src_right, tgt_embed, tgt_left, tgt_right, stay=6,
    )
    src = exchange(src, COL).reshape(rank, 3 * n)
    tgt = lax.all_gather(tgt, ROW, axis=0, tiled=True)
    src_logit, tgt_logit = src_logit.reshape(1, n), tgt_logit.reshape(1, m)
    src_weight, tgt_weight = src_weight.reshape(nt, LANES), tgt_weight.reshape(mt, LANES)

    (part,) = call(
        opening_kernel,
        [((row_peers, CHUNK, LANES), F32)],
        [
            ((rank + PAD, n), BF16),
            ((rank + PAD, m), BF16),
            ((2 * rank + PAD, m), BF16),
            ((1, n), F32),
            ((1, m), F32),
            ((nt, LANES), F32),
            ((mt, LANES), F32),
            pltpu.SemaphoreType.DMA((4,)),
        ],
        src, tgt, src_logit, tgt_logit, src_weight, tgt_weight, stay=4, room=32,
    )
    (part,) = call(relay_kernel, [((col_peers, CHUNK, LANES), F32)], [], exchange(part, ROW))
    (part,) = call(relay_kernel, [((row_peers, CHUNK, LANES), F32)], [], exchange(part, COL))
    kernel, part, row_mass, col_mass = call(
        functools.partial(tile_kernel, mass_scale, row_peers, col_peers),
        [
            ((n, m), BF16),
            ((col_peers, nt, LANES), BF16),
            ((nt, LANES), F32),
            ((mt, LANES), F32),
        ],
        [
            ((2 * rank + PAD, n), BF16),
            ((2 * rank + PAD, m), BF16),
            ((nt, LANES), F32),
            ((half, LANES), F32),
            ((1, n), F32),
            ((1, m), F32),
            ((nt, LANES), F32),
            ((mt, LANES), F32),
            pltpu.SemaphoreType.DMA((4,)),
        ],
        exchange(part, ROW), src, tgt, src_logit, tgt_logit, src_weight, tgt_weight,
        stay=4, room=32,
    )
    for sweep in range(SWEEPS):
        row_scale, part = call(
            functools.partial(sweep_kernel, True),
            [((nt, LANES), F32), ((row_peers, mt, LANES), BF16)],
            [((8, n), F32), ((mt, LANES), F32)],
            exchange(part, COL), row_mass, kernel,
        )
        part = exchange(part, ROW)
        if sweep + 1 < SWEEPS:
            _, part = call(
                functools.partial(sweep_kernel, False),
                [((mt, LANES), F32), ((col_peers, nt, LANES), BF16)],
                [((8, m), F32), ((nt, LANES), F32)],
                part, col_mass, kernel,
            )
    row_potential, side = call(
        functools.partial(side_kernel, math.log(n_all) + math.log(m_all)),
        [((nt, LANES), F32), ((rank, m), F32)],
        [((8, n), F32)],
        row_scale, kernel, src,
    )
    col_potential, part = call(
        closing_kernel,
        [((mt, LANES), F32), ((row_peers, half, LANES), BF16)],
        [((8, m), F32), ((2 * rank, m), BF16)],
        part, col_mass, side, tgt,
    )
    (part,) = call(relay_kernel, [((col_peers, half, LANES), BF16)], [], exchange(part, ROW))
    (new_core,) = call(
        functools.partial(final_kernel, mass_scale), [((rank, rank), F32)], [], exchange(part, COL)
    )
    return (row_potential.reshape(n), col_potential.reshape(m), new_core)


def solution(mesh):
    torus = Mesh(mesh.devices.reshape(8, 2, 8, 4), ("row_0", "row_1", "col_0", "col_1"))
    placed = (
        P(COL, ROW),
        P(COL, ROW),
        P(COL, ROW),
        P(ROW),
        P(ROW),
        P(ROW, COL),
        P(ROW, COL),
        P(ROW, COL),
        P(COL),
        P(COL),
    )
    return jax.shard_map(
        body, mesh=torus, in_specs=placed, out_specs=(P(ROW), P(COL), P()), check_vma=False
    )
```

```python
import functools
import math

import jax
import jax.numpy as jnp
from jax import lax
from jax.experimental import pallas as pl
from jax.experimental.pallas import tpu as pltpu
from jax.sharding import Mesh
from jax.sharding import PartitionSpec as P

SWEEPS = 3
ROW = ("row_0", "row_1", "core")
NEAR = ("row_1", "core")
COL = ("col_0", "col_1")
F32 = jnp.float32
BF16 = jnp.bfloat16
LANES = 128
PAD = 16

VMEM = pl.BlockSpec(memory_space=pltpu.VMEM)
HBM = pl.BlockSpec(memory_space=pltpu.HBM)
FIRST = (((0,), (0,)), ((), ()))
LAST = (((1,), (1,)), ((), ()))
PLAIN = (((1,), (0,)), ((), ()))


def dot(a, b, dims):
    return lax.dot_general(a, b, dims, preferred_element_type=F32)


def three_parts(v):
    high = v.astype(BF16).astype(F32)
    rest = v - high
    mid = rest.astype(BF16).astype(F32)
    low = (rest - mid).astype(BF16).astype(F32)
    return high, mid, low


def in_parts(a, b):
    rows = a.shape[0]
    total = dot(jnp.concatenate(three_parts(a), axis=0).astype(BF16), b, LAST)
    return total[:rows] + total[rows : 2 * rows] + total[2 * rows :]


def logit_rows(v, first):
    n = v.shape[1]
    row = lax.broadcasted_iota(jnp.int32, (PAD, n), 0)
    at, ones = (0, 3) if first else (3, 0)
    out = jnp.where((row >= ones) & (row < ones + 3), 1.0, 0.0)
    for index, part in enumerate(three_parts(v)):
        out = jnp.where(row == at + index, jnp.broadcast_to(part, (PAD, n)), out)
    return out.astype(BF16)


def to_lanes(v, flat_ref):
    for s in range(v.shape[0]):
        flat_ref[:, s * LANES : (s + 1) * LANES] = jnp.broadcast_to(v[s : s + 1], (8, LANES))
    return flat_ref[...]


def to_tiles(row, tile_ref):
    for s in range(tile_ref.shape[0]):
        tile_ref[s : s + 1, :] = row[:, s * LANES : (s + 1) * LANES]
    return tile_ref[...]


def over_lanes(v):
    width = v.shape[1]
    total = v[:, :LANES]
    for s in range(1, width // LANES):
        total = total + v[:, s * LANES : (s + 1) * LANES]
    ones = jnp.ones((PAD, LANES), BF16)
    return sum(dot(ones, part.astype(BF16), LAST)[0:1] for part in three_parts(total))


def send(out_ref, v):
    v = v.astype(out_ref.dtype)
    for p in range(out_ref.shape[0]):
        out_ref[p] = v


def received(ref):
    total = ref[0].astype(F32)
    for p in range(1, ref.shape[0]):
        total = total + ref[p].astype(F32)
    return total


def halves_on_lanes(core, rank):
    half = rank // 2
    lane = lax.broadcasted_iota(jnp.int32, (half, 2 * rank), 1)
    return jnp.where(lane < rank, core[:half], core[half:rank])


def fetch(there, here, sem):
    copies = [pltpu.make_async_copy(t, h, sem.at[k]) for k, (t, h) in enumerate(zip(there, here))]
    for copy in copies:
        copy.start()
    return copies


def pack_kernel(*refs):
    there, (src_out, tgt_out), here, sem = refs[:6], refs[6:8], refs[8:14], refs[14]
    for copy in fetch(there, here, sem):
        copy.wait()
    mine = jnp.concatenate([ref[...] for ref in here[:3]], axis=1)
    for p in range(src_out.shape[0]):
        src_out[p] = mine
    tgt_out[...] = jnp.concatenate([ref[...] for ref in here[3:]], axis=1)


def opening_kernel(
    src, tgt, src_logit_in, tgt_logit_in, src_weight_in, tgt_weight_in, out,
    xs, xt, right, src_logit, tgt_logit, src_weight, tgt_weight, flat, sem,
):
    copies = fetch(
        (src_logit_in, tgt_logit_in, src_weight_in, tgt_weight_in),
        (src_logit, tgt_logit, src_weight, tgt_weight),
        sem,
    )
    rank = src.shape[0]
    n = src_logit.shape[1]
    m = tgt_logit.shape[1]
    xs[:rank] = (src[:, :n].astype(F32) * 0.125).astype(BF16)
    xt[:rank] = tgt[:, :m]
    right[:rank] = tgt[:, 2 * m :]
    right[rank : 2 * rank] = tgt[:, 2 * m :]
    row = lax.broadcasted_iota(jnp.int32, (PAD, m), 0)
    right[2 * rank :] = jnp.where(row == 0, 1.0, 0.0).astype(BF16)
    for copy in copies:
        copy.wait()
    xs[rank:] = logit_rows(src_logit[...], True)
    xt[rank:] = logit_rows(tgt_logit[...], False)
    tile = jnp.exp(dot(xs[...], xt[...], FIRST)).astype(BF16)
    row = lax.broadcasted_iota(jnp.int32, (PAD, n), 0)
    left = jnp.concatenate([src[:, 2 * n :], jnp.where(row == 0, 1.0, 0.0).astype(BF16)], axis=0)
    both = in_parts(dot(left, tile, PLAIN), right[...])
    core = halves_on_lanes(both[:, : 2 * rank], rank)
    total = both[rank : rank + 1, 2 * rank : 2 * rank + 1]
    src_sum = jnp.sum(src_weight[...], keepdims=True)
    tgt_sum = jnp.sum(tgt_weight[...], keepdims=True)
    lane = lax.broadcasted_iota(jnp.int32, (1, LANES), 1)
    sums = jnp.where(
        lane == 0, total, jnp.where(lane == 1, src_sum, jnp.where(lane == 2, tgt_sum, 0.0))
    )
    parts, _, width = flat.shape
    for q in range(parts):
        for s in range(width // LANES - 1):
            k = q * (width // LANES - 1) + s
            flat[q, :, s * LANES : (s + 1) * LANES] = core[k : k + 1]
        flat[q, :, width - LANES :] = sums
    for p in range(out.shape[0]):
        out[p] = flat[p % parts]


def relay_kernel(y, out):
    send(out, received(y))


def tile_kernel(
    mass_scale, row_peers, col_peers,
    z, src, tgt, src_logit_in, tgt_logit_in, src_weight_in, tgt_weight_in,
    kernel, flipped, out, row_mass, col_mass,
    xs, xt, tiles, core, src_logit, tgt_logit, src_weight, tgt_weight, sem,
):
    copies = fetch(
        (src_logit_in, tgt_logit_in, src_weight_in, tgt_weight_in),
        (src_logit, tgt_logit, src_weight, tgt_weight),
        sem,
    )
    rank = src.shape[0]
    half = rank // 2
    n = src_logit.shape[1]
    m = tgt_logit.shape[1]
    parts, _, width = z.shape
    for q in range(parts):
        for s in range(width // LANES - 1):
            k = q * (width // LANES - 1) + s
            core[k : k + 1] = z[q, :, s * LANES : (s + 1) * LANES]
    sums = z[0, :, width - LANES :]
    grand_total = sums[:, 0:1]
    mixing = mass_scale * core[...] / grand_total
    parts = jnp.concatenate(three_parts(mixing), axis=0).astype(BF16)
    top = src[:half, n : 2 * n]
    bottom = src[half:, n : 2 * n]
    top = dot(parts, jnp.concatenate([top, top, top], axis=0), FIRST)
    bottom = dot(parts, jnp.concatenate([bottom, bottom, bottom], axis=0), FIRST)
    xs[:rank] = (src[:, :n].astype(F32) * 0.125).astype(BF16)
    xs[rank : 2 * rank] = (2.0 * (top[:rank] + bottom[rank:])).astype(BF16)
    for copy in copies:
        copy.wait()
    row_mass[...] = src_weight[...] / (sums[:, 1:2] / col_peers)
    col_mass[...] = tgt_weight[...] / (sums[:, 2:3] / row_peers)
    xs[2 * rank :] = logit_rows(src_logit[...], True)
    xt[:rank] = tgt[:, :m]
    xt[rank : 2 * rank] = tgt[:, m : 2 * m]
    xt[2 * rank :] = logit_rows(tgt_logit[...] - jnp.log(grand_total), False)
    tile = jnp.exp(dot(xs[...], xt[...], FIRST)).astype(BF16)
    kernel[...] = tile
    flipped[...] = tile.T
    send(out, to_tiles(over_lanes(tile.astype(F32)), tiles))


def sweep_kernel(y, mass, kernel, out, *rest):
    *scale, flat, tiles = rest
    s = mass[...] / received(y)
    for ref in scale:
        ref[...] = s
    weights = to_lanes(s, flat).astype(BF16)
    send(out, to_tiles(dot(weights, kernel[...], PLAIN)[0:1], tiles))


def side_kernel(shift, row_scale, kernel, src, row_potential, side, flat):
    rank = src.shape[0]
    n = kernel.shape[0]
    row_potential[...] = jnp.log(row_scale[...]) + shift
    rows = to_lanes(row_scale[...], flat)
    left = src[:, 2 * n :].astype(F32) * rows[0:1]
    parts = jnp.concatenate(three_parts(left), axis=0).astype(BF16)
    total = dot(parts, kernel[...], PLAIN)
    side[...] = total[:rank] + total[rank : 2 * rank] + total[2 * rank :]


def closing_kernel(y, mass, side, tgt, col_potential, out, flat, twice, potential, sem):
    rank, m = side.shape
    col_scale = mass[...] / received(y)
    potential[...] = jnp.log(col_scale)
    (copy,) = fetch([potential], [col_potential], sem)
    cols = to_lanes(col_scale, flat)
    scaled = (tgt[:, 2 * m :].astype(F32) * cols[0:1]).astype(BF16)
    twice[:rank] = scaled
    twice[rank:] = scaled
    send(out, halves_on_lanes(in_parts(side[...], twice[...]), rank))
    copy.wait()


def final_kernel(mass_scale, y, out):
    core = mass_scale * received(y)
    half, rank = core.shape[0], core.shape[1] // 2
    out[:half] = core[:, :rank]
    out[half:] = core[:, rank:]


def call(body, outs, scratch, *args, stay=0, out_stay=0, room=8):
    here, there = args[: len(args) - stay], args[len(args) - stay :]
    there = [pltpu.with_memory_space_constraint(a, pltpu.HBM) for a in there]
    return pl.pallas_call(
        body,
        out_shape=[jax.ShapeDtypeStruct(s, d) for s, d in outs],
        in_specs=[VMEM] * (len(args) - stay) + [HBM] * stay,
        out_specs=[HBM] * out_stay + [VMEM] * (len(outs) - out_stay),
        scratch_shapes=[pltpu.VMEM(*x) if isinstance(x, tuple) else x for x in scratch],
        compiler_params=pltpu.CompilerParams(vmem_limit_bytes=room << 20),
    )(*here, *there)


def exchange(value, axis):
    return lax.all_to_all(value, axis, 0, 0, tiled=True)


def body(
    src_embed,
    src_left,
    src_right,
    src_logit,
    src_weight,
    tgt_embed,
    tgt_left,
    tgt_right,
    tgt_logit,
    tgt_weight,
):
    n, m = src_logit.shape[0], tgt_logit.shape[0]
    row_peers, col_peers = lax.axis_size(ROW), lax.axis_size(COL)
    n_all, m_all = n * row_peers, m * col_peers
    rank = src_embed.shape[0] * col_peers
    half = rank // 2
    mass_scale = math.sqrt(n_all * m_all)
    nt, mt = n // LANES, m // LANES

    src, tgt = call(
        pack_kernel,
        [
            ((col_peers, rank // col_peers, 3 * n), BF16),
            ((rank // row_peers, 3 * m), BF16),
        ],
        [
            *[(a.shape, BF16) for a in (src_embed, src_left, src_right)],
            *[(a.shape, BF16) for a in (tgt_embed, tgt_left, tgt_right)],
            pltpu.SemaphoreType.DMA((6,)),
        ],
        src_embed, src_left, src_right, tgt_embed, tgt_left, tgt_right, stay=6,
    )
    src = exchange(src, COL).reshape(rank, 3 * n)
    tgt = lax.all_gather(tgt, ROW, axis=0, tiled=True)
    src_logit, tgt_logit = src_logit.reshape(1, n), tgt_logit.reshape(1, m)
    src_weight, tgt_weight = src_weight.reshape(nt, LANES), tgt_weight.reshape(mt, LANES)

    near = lax.axis_size(NEAR)
    width = half * LANES // near + LANES
    (part,) = call(
        opening_kernel,
        [((row_peers, 1, width), F32)],
        [
            ((rank + PAD, n), BF16),
            ((rank + PAD, m), BF16),
            ((2 * rank + PAD, m), BF16),
            ((1, n), F32),
            ((1, m), F32),
            ((nt, LANES), F32),
            ((mt, LANES), F32),
            ((near, 1, width), F32),
            pltpu.SemaphoreType.DMA((4,)),
        ],
        src, tgt, src_logit, tgt_logit, src_weight, tgt_weight, stay=4, room=32,
    )
    (part,) = call(relay_kernel, [((col_peers, 1, width), F32)], [], exchange(part, ROW))
    (part,) = call(relay_kernel, [((near, 1, width), F32)], [], exchange(part, COL))
    kernel, flipped, part, row_mass, col_mass = call(
        functools.partial(tile_kernel, mass_scale, row_peers, col_peers),
        [
            ((n, m), BF16),
            ((m, n), BF16),
            ((col_peers, nt, LANES), BF16),
            ((nt, LANES), F32),
            ((mt, LANES), F32),
        ],
        [
            ((2 * rank + PAD, n), BF16),
            ((2 * rank + PAD, m), BF16),
            ((nt, LANES), F32),
            ((half, LANES), F32),
            ((1, n), F32),
            ((1, m), F32),
            ((nt, LANES), F32),
            ((mt, LANES), F32),
            pltpu.SemaphoreType.DMA((4,)),
        ],
        exchange(part, NEAR), src, tgt, src_logit, tgt_logit, src_weight, tgt_weight,
        stay=4, room=32,
    )
    for sweep in range(SWEEPS):
        last = sweep + 1 == SWEEPS
        part, *row_scale = call(
            sweep_kernel,
            [((row_peers, mt, LANES), BF16), ((nt, LANES), F32)][: 1 + last],
            [((8, n), F32), ((mt, LANES), F32)],
            exchange(part, COL), row_mass, kernel,
        )
        part = exchange(part, ROW)
        if not last:
            (part,) = call(
                sweep_kernel,
                [((col_peers, nt, LANES), BF16)],
                [((8, m), F32), ((nt, LANES), F32)],
                part, col_mass, flipped,
            )
    (row_scale,) = row_scale
    row_potential, side = call(
        functools.partial(side_kernel, math.log(n_all) + math.log(m_all)),
        [((nt, LANES), F32), ((rank, m), F32)],
        [((8, n), F32)],
        row_scale, kernel, src,
    )
    col_potential, part = call(
        closing_kernel,
        [((mt, LANES), F32), ((row_peers, half, LANES), BF16)],
        [((8, m), F32), ((2 * rank, m), BF16), ((mt, LANES), F32), pltpu.SemaphoreType.DMA((1,))],
        part, col_mass, side, tgt, out_stay=1,
    )
    (part,) = call(relay_kernel, [((col_peers, half, LANES), BF16)], [], exchange(part, ROW))
    (new_core,) = call(
        functools.partial(final_kernel, mass_scale), [((rank, rank), F32)], [], exchange(part, COL)
    )
    return (row_potential.reshape(n), col_potential.reshape(m), new_core)


def solution(mesh):
    torus = Mesh(mesh.devices.reshape(4, 2, 2, 8, 4), ("row_0", "row_1", "core", "col_0", "col_1"))
    placed = (
        P(COL, ROW),
        P(COL, ROW),
        P(COL, ROW),
        P(ROW),
        P(ROW),
        P(ROW, COL),
        P(ROW, COL),
        P(ROW, COL),
        P(COL),
        P(COL),
    )
    return jax.shard_map(
        body, mesh=torus, in_specs=placed, out_specs=(P(ROW), P(COL), P()), check_vma=False
    )
```

```python
import functools
import math

import jax
import jax.numpy as jnp
from jax import lax
from jax.experimental import pallas as pl
from jax.experimental.pallas import tpu as pltpu
from jax.sharding import Mesh
from jax.sharding import PartitionSpec as P

SWEEPS = 3
ROW = ("row_0", "row_1", "core")
NEAR = ("row_1", "core")
COL = ("col_0", "col_1")
F32 = jnp.float32
BF16 = jnp.bfloat16
LANES = 128
PAD = 16

VMEM = pl.BlockSpec(memory_space=pltpu.VMEM)
HBM = pl.BlockSpec(memory_space=pltpu.HBM)
FIRST = (((0,), (0,)), ((), ()))
LAST = (((1,), (1,)), ((), ()))
PLAIN = (((1,), (0,)), ((), ()))


def dot(a, b, dims):
    return lax.dot_general(a, b, dims, preferred_element_type=F32)


def three_parts(v):
    high = v.astype(BF16).astype(F32)
    rest = v - high
    mid = rest.astype(BF16).astype(F32)
    low = (rest - mid).astype(BF16).astype(F32)
    return high, mid, low


def in_parts(a, b):
    rows = a.shape[0]
    total = dot(jnp.concatenate(three_parts(a), axis=0).astype(BF16), b, LAST)
    return total[:rows] + total[rows : 2 * rows] + total[2 * rows :]


def logit_rows(v, first):
    n = v.shape[1]
    row = lax.broadcasted_iota(jnp.int32, (PAD, n), 0)
    at, ones = (0, 3) if first else (3, 0)
    out = jnp.where((row >= ones) & (row < ones + 3), 1.0, 0.0)
    for index, part in enumerate(three_parts(v)):
        out = jnp.where(row == at + index, jnp.broadcast_to(part, (PAD, n)), out)
    return out.astype(BF16)


def to_lanes(v, flat_ref):
    for s in range(v.shape[0]):
        flat_ref[:, s * LANES : (s + 1) * LANES] = jnp.broadcast_to(v[s : s + 1], (8, LANES))
    return flat_ref[...]


def to_tiles(row, tile_ref):
    for s in range(tile_ref.shape[0]):
        tile_ref[s : s + 1, :] = row[:, s * LANES : (s + 1) * LANES]
    return tile_ref[...]


def send(out_ref, v):
    v = v.astype(out_ref.dtype)
    for p in range(out_ref.shape[0]):
        out_ref[p] = v


def received(ref):
    total = ref[0].astype(F32)
    for p in range(1, ref.shape[0]):
        total = total + ref[p].astype(F32)
    return total


def halves_on_lanes(core, rank):
    half = rank // 2
    lane = lax.broadcasted_iota(jnp.int32, (half, 2 * rank), 1)
    return jnp.where(lane < rank, core[:half], core[half:rank])


def fetch(there, here, sem):
    copies = [pltpu.make_async_copy(t, h, sem.at[k]) for k, (t, h) in enumerate(zip(there, here))]
    for copy in copies:
        copy.start()
    return copies


def pack_kernel(*refs):
    there, (src_out, tgt_out), here, sem = refs[:6], refs[6:8], refs[8:14], refs[14]
    for copy in fetch(there, here, sem):
        copy.wait()
    mine = jnp.concatenate([ref[...] for ref in here[:3]], axis=1)
    for p in range(src_out.shape[0]):
        src_out[p] = mine
    tgt_out[...] = jnp.concatenate([ref[...] for ref in here[3:]], axis=1)


def opening_kernel(
    src, tgt, src_logit_in, tgt_logit_in, src_weight_in, tgt_weight_in, out,
    xs, xt, right, src_logit, tgt_logit, src_weight, tgt_weight, flat, sem,
):
    copies = fetch(
        (src_logit_in, tgt_logit_in, src_weight_in, tgt_weight_in),
        (src_logit, tgt_logit, src_weight, tgt_weight),
        sem,
    )
    rank = src.shape[0]
    n = src_logit.shape[1]
    m = tgt_logit.shape[1]
    xs[:rank] = (src[:, :n].astype(F32) * 0.125).astype(BF16)
    xt[:rank] = tgt[:, :m]
    right[:rank] = tgt[:, 2 * m :]
    right[rank : 2 * rank] = tgt[:, 2 * m :]
    row = lax.broadcasted_iota(jnp.int32, (PAD, m), 0)
    right[2 * rank :] = jnp.where(row == 0, 1.0, 0.0).astype(BF16)
    for copy in copies:
        copy.wait()
    xs[rank:] = logit_rows(src_logit[...], True)
    xt[rank:] = logit_rows(tgt_logit[...], False)
    row = lax.broadcasted_iota(jnp.int32, (PAD, n), 0)
    left = jnp.concatenate([src[:, 2 * n :], jnp.where(row == 0, 1.0, 0.0).astype(BF16)], axis=0)
    tile = jnp.exp(dot(xs[...], xt[...], FIRST)).astype(BF16)
    side = dot(left, tile, PLAIN)
    both = in_parts(side, right[...])
    core = halves_on_lanes(both[:, : 2 * rank], rank)
    total = both[rank : rank + 1, 2 * rank : 2 * rank + 1]
    src_sum = jnp.sum(src_weight[...], keepdims=True)
    tgt_sum = jnp.sum(tgt_weight[...], keepdims=True)
    lane = lax.broadcasted_iota(jnp.int32, (1, LANES), 1)
    sums = jnp.where(
        lane == 0, total, jnp.where(lane == 1, src_sum, jnp.where(lane == 2, tgt_sum, 0.0))
    )
    parts, _, width = flat.shape
    for q in range(parts):
        for s in range(width // LANES - 1):
            k = q * (width // LANES - 1) + s
            flat[q, :, s * LANES : (s + 1) * LANES] = core[k : k + 1]
        flat[q, :, width - LANES :] = sums
    for p in range(out.shape[0]):
        out[p] = flat[p % parts]


def relay_kernel(y, out):
    send(out, received(y))


def tile_kernel(
    mass_scale, row_peers, col_peers,
    z, src, tgt, src_logit_in, tgt_logit_in, src_weight_in, tgt_weight_in,
    kernel, flipped, out, row_mass, col_mass,
    xs, xt, totals, tiles, core, src_logit, tgt_logit, src_weight, tgt_weight, sem,
):
    copies = fetch(
        (src_logit_in, tgt_logit_in, src_weight_in, tgt_weight_in),
        (src_logit, tgt_logit, src_weight, tgt_weight),
        sem,
    )
    rank = src.shape[0]
    half = rank // 2
    n = src_logit.shape[1]
    m = tgt_logit.shape[1]
    parts, _, width = z.shape
    for q in range(parts):
        for s in range(width // LANES - 1):
            k = q * (width // LANES - 1) + s
            core[k : k + 1] = z[q, :, s * LANES : (s + 1) * LANES]
    sums = z[0, :, width - LANES :]
    grand_total = sums[:, 0:1]
    mixing = mass_scale * core[...] / grand_total
    parts = jnp.concatenate(three_parts(mixing), axis=0).astype(BF16)
    top = src[:half, n : 2 * n]
    bottom = src[half:, n : 2 * n]
    top = dot(parts, jnp.concatenate([top, top, top], axis=0), FIRST)
    bottom = dot(parts, jnp.concatenate([bottom, bottom, bottom], axis=0), FIRST)
    xs[:rank] = (src[:, :n].astype(F32) * 0.125).astype(BF16)
    xs[rank : 2 * rank] = (2.0 * (top[:rank] + bottom[rank:])).astype(BF16)
    for copy in copies:
        copy.wait()
    row_mass[...] = src_weight[...] / (sums[:, 1:2] / col_peers)
    col_mass[...] = tgt_weight[...] / (sums[:, 2:3] / row_peers)
    xs[2 * rank :] = logit_rows(src_logit[...], True)
    xt[:rank] = tgt[:, :m]
    xt[rank : 2 * rank] = tgt[:, m : 2 * m]
    xt[2 * rank :] = logit_rows(tgt_logit[...] - jnp.log(grand_total), False)
    tile = jnp.exp(dot(xs[...], xt[...], FIRST)).astype(BF16)
    kernel[...] = tile
    turned = tile.T
    flipped[...] = turned
    totals[...] = dot(jnp.ones((8, m), BF16), turned, PLAIN)
    send(out, to_tiles(totals[0:1], tiles))


def sweep_kernel(y, mass, kernel, out, *rest):
    *scale, flat, tiles = rest
    s = mass[...] / received(y)
    for ref in scale:
        ref[...] = s
    weights = to_lanes(s, flat).astype(BF16)
    send(out, to_tiles(dot(weights, kernel[...], PLAIN)[0:1], tiles))


def side_kernel(shift, row_scale, src, kernel, row_potential, side, flat, tile, sem):
    rank = src.shape[0]
    slabs, rows, _ = tile.shape
    n = slabs * rows
    copies = fetch(
        [kernel.at[pl.ds(k * rows, rows)] for k in range(slabs)],
        [tile.at[k] for k in range(slabs)],
        sem,
    )
    row_potential[...] = jnp.log(row_scale[...]) + shift
    scale = to_lanes(row_scale[...], flat)
    left = src[:, 2 * n :].astype(F32) * scale[0:1]
    parts = jnp.concatenate(three_parts(left), axis=0).astype(BF16)
    total = 0.0
    for k, copy in enumerate(copies):
        copy.wait()
        total = total + dot(parts[:, k * rows : (k + 1) * rows], tile[k], PLAIN)
    side[...] = total[:rank] + total[rank : 2 * rank] + total[2 * rank :]


def closing_kernel(y, mass, side, tgt, col_potential, out, flat, twice, potential, sem):
    rank, m = side.shape
    col_scale = mass[...] / received(y)
    potential[...] = jnp.log(col_scale)
    (copy,) = fetch([potential], [col_potential], sem)
    cols = to_lanes(col_scale, flat)
    scaled = (tgt[:, 2 * m :].astype(F32) * cols[0:1]).astype(BF16)
    twice[:rank] = scaled
    twice[rank:] = scaled
    send(out, halves_on_lanes(in_parts(side[...], twice[...]), rank))
    copy.wait()


def final_kernel(mass_scale, y, out):
    core = mass_scale * received(y)
    half, rank = core.shape[0], core.shape[1] // 2
    out[:half] = core[:, :rank]
    out[half:] = core[:, rank:]


def call(body, outs, scratch, *args, stay=0, out_stay=0, room=8):
    here, there = args[: len(args) - stay], args[len(args) - stay :]
    there = [pltpu.with_memory_space_constraint(a, pltpu.HBM) for a in there]
    return pl.pallas_call(
        body,
        out_shape=[jax.ShapeDtypeStruct(s, d) for s, d in outs],
        in_specs=[VMEM] * (len(args) - stay) + [HBM] * stay,
        out_specs=[HBM] * out_stay + [VMEM] * (len(outs) - out_stay),
        scratch_shapes=[pltpu.VMEM(*x) if isinstance(x, tuple) else x for x in scratch],
        compiler_params=pltpu.CompilerParams(vmem_limit_bytes=room << 20),
    )(*here, *there)


def exchange(value, axis):
    return lax.all_to_all(value, axis, 0, 0, tiled=True)


def body(
    src_embed,
    src_left,
    src_right,
    src_logit,
    src_weight,
    tgt_embed,
    tgt_left,
    tgt_right,
    tgt_logit,
    tgt_weight,
):
    n, m = src_logit.shape[0], tgt_logit.shape[0]
    row_peers, col_peers = lax.axis_size(ROW), lax.axis_size(COL)
    n_all, m_all = n * row_peers, m * col_peers
    rank = src_embed.shape[0] * col_peers
    half = rank // 2
    mass_scale = math.sqrt(n_all * m_all)
    nt, mt = n // LANES, m // LANES

    src, tgt = call(
        pack_kernel,
        [
            ((col_peers, rank // col_peers, 3 * n), BF16),
            ((rank // row_peers, 3 * m), BF16),
        ],
        [
            *[(a.shape, BF16) for a in (src_embed, src_left, src_right)],
            *[(a.shape, BF16) for a in (tgt_embed, tgt_left, tgt_right)],
            pltpu.SemaphoreType.DMA((6,)),
        ],
        src_embed, src_left, src_right, tgt_embed, tgt_left, tgt_right, stay=6,
    )
    src = exchange(src, COL).reshape(rank, 3 * n)
    tgt = lax.all_gather(tgt, ROW, axis=0, tiled=True)
    src_logit, tgt_logit = src_logit.reshape(1, n), tgt_logit.reshape(1, m)
    src_weight, tgt_weight = src_weight.reshape(nt, LANES), tgt_weight.reshape(mt, LANES)

    near = lax.axis_size(NEAR)
    width = half * LANES // near + LANES
    (part,) = call(
        opening_kernel,
        [((row_peers, 1, width), F32)],
        [
            ((rank + PAD, n), BF16),
            ((rank + PAD, m), BF16),
            ((2 * rank + PAD, m), BF16),
            ((1, n), F32),
            ((1, m), F32),
            ((nt, LANES), F32),
            ((mt, LANES), F32),
            ((near, 1, width), F32),
            pltpu.SemaphoreType.DMA((4,)),
        ],
        src, tgt, src_logit, tgt_logit, src_weight, tgt_weight, stay=4, room=32,
    )
    (part,) = call(relay_kernel, [((col_peers, 1, width), F32)], [], exchange(part, ROW))
    (part,) = call(relay_kernel, [((near, 1, width), F32)], [], exchange(part, COL))
    kernel, flipped, part, row_mass, col_mass = call(
        functools.partial(tile_kernel, mass_scale, row_peers, col_peers),
        [
            ((n, m), BF16),
            ((m, n), BF16),
            ((col_peers, nt, LANES), BF16),
            ((nt, LANES), F32),
            ((mt, LANES), F32),
        ],
        [
            ((2 * rank + PAD, n), BF16),
            ((2 * rank + PAD, m), BF16),
            ((8, n), F32),
            ((nt, LANES), F32),
            ((half, LANES), F32),
            ((1, n), F32),
            ((1, m), F32),
            ((nt, LANES), F32),
            ((mt, LANES), F32),
            pltpu.SemaphoreType.DMA((4,)),
        ],
        exchange(part, NEAR), src, tgt, src_logit, tgt_logit, src_weight, tgt_weight,
        stay=4, room=32,
    )
    for sweep in range(SWEEPS):
        last = sweep + 1 == SWEEPS
        part, *row_scale = call(
            sweep_kernel,
            [((row_peers, mt, LANES), BF16), ((nt, LANES), F32)][: 1 + last],
            [((8, n), F32), ((mt, LANES), F32)],
            exchange(part, COL), row_mass, kernel,
        )
        part = exchange(part, ROW)
        if not last:
            (part,) = call(
                sweep_kernel,
                [((col_peers, nt, LANES), BF16)],
                [((8, m), F32), ((nt, LANES), F32)],
                part, col_mass, flipped,
            )
    (row_scale,) = row_scale
    row_potential, side = call(
        functools.partial(side_kernel, math.log(n_all) + math.log(m_all)),
        [((nt, LANES), F32), ((rank, m), F32)],
        [((8, n), F32), ((8, n // 8, m), BF16), pltpu.SemaphoreType.DMA((8,))],
        row_scale, src, kernel, stay=1, room=16,
    )
    col_potential, part = call(
        closing_kernel,
        [((mt, LANES), F32), ((row_peers, half, LANES), BF16)],
        [((8, m), F32), ((2 * rank, m), BF16), ((mt, LANES), F32), pltpu.SemaphoreType.DMA((1,))],
        part, col_mass, side, tgt, out_stay=1,
    )
    (part,) = call(relay_kernel, [((col_peers, half, LANES), BF16)], [], exchange(part, ROW))
    (new_core,) = call(
        functools.partial(final_kernel, mass_scale), [((rank, rank), F32)], [], exchange(part, COL)
    )
    return (row_potential.reshape(n), col_potential.reshape(m), new_core)


def solution(mesh):
    torus = Mesh(mesh.devices.reshape(4, 2, 2, 8, 4), ("row_0", "row_1", "core", "col_0", "col_1"))
    placed = (
        P(COL, ROW),
        P(COL, ROW),
        P(COL, ROW),
        P(ROW),
        P(ROW),
        P(ROW, COL),
        P(ROW, COL),
        P(ROW, COL),
        P(COL),
        P(COL),
    )
    return jax.shard_map(
        body, mesh=torus, in_specs=placed, out_specs=(P(ROW), P(COL), P()), check_vma=False
    )
```

```python
import functools
import math

import jax
import jax.numpy as jnp
from jax import lax
from jax.experimental import pallas as pl
from jax.experimental.pallas import tpu as pltpu
from jax.sharding import Mesh
from jax.sharding import PartitionSpec as P

SWEEPS = 3
ROW = ("row_0", "row_1", "core")
NEAR = ("row_1", "core")
COL = ("col_0", "col_1")
F32 = jnp.float32
BF16 = jnp.bfloat16
LANES = 128
PAD = 16

VMEM = pl.BlockSpec(memory_space=pltpu.VMEM)
HBM = pl.BlockSpec(memory_space=pltpu.HBM)
FIRST = (((0,), (0,)), ((), ()))
LAST = (((1,), (1,)), ((), ()))
PLAIN = (((1,), (0,)), ((), ()))


def dot(a, b, dims):
    return lax.dot_general(a, b, dims, preferred_element_type=F32)


def three_parts(v):
    high = v.astype(BF16).astype(F32)
    rest = v - high
    mid = rest.astype(BF16).astype(F32)
    low = (rest - mid).astype(BF16).astype(F32)
    return high, mid, low


def in_parts(a, b):
    rows = a.shape[0]
    total = dot(jnp.concatenate(three_parts(a), axis=0).astype(BF16), b, LAST)
    return total[:rows] + total[rows : 2 * rows] + total[2 * rows :]


def logit_rows(v, first):
    n = v.shape[1]
    row = lax.broadcasted_iota(jnp.int32, (PAD, n), 0)
    at, ones = (0, 3) if first else (3, 0)
    out = jnp.where((row >= ones) & (row < ones + 3), 1.0, 0.0)
    for index, part in enumerate(three_parts(v)):
        out = jnp.where(row == at + index, jnp.broadcast_to(part, (PAD, n)), out)
    return out.astype(BF16)


def to_lanes(v, flat_ref):
    for s in range(v.shape[0]):
        flat_ref[:, s * LANES : (s + 1) * LANES] = jnp.broadcast_to(v[s : s + 1], (8, LANES))
    return flat_ref[...]


def to_tiles(row, tile_ref):
    for s in range(tile_ref.shape[0]):
        tile_ref[s : s + 1, :] = row[:, s * LANES : (s + 1) * LANES]
    return tile_ref[...]


def send(out_ref, v):
    v = v.astype(out_ref.dtype)
    for p in range(out_ref.shape[0]):
        out_ref[p] = v


def received(ref):
    total = ref[0].astype(F32)
    for p in range(1, ref.shape[0]):
        total = total + ref[p].astype(F32)
    return total


def halves_on_lanes(core, rank):
    half = rank // 2
    lane = lax.broadcasted_iota(jnp.int32, (half, 2 * rank), 1)
    return jnp.where(lane < rank, core[:half], core[half:rank])


def fetch(there, here, sem):
    copies = [pltpu.make_async_copy(t, h, sem.at[k]) for k, (t, h) in enumerate(zip(there, here))]
    for copy in copies:
        copy.start()
    return copies


def pack_kernel(*refs):
    there, (src_out, tgt_out), here, sem = refs[:6], refs[6:8], refs[8:14], refs[14]
    for copy in fetch(there, here, sem):
        copy.wait()
    mine = jnp.concatenate([ref[...] for ref in here[:3]], axis=1)
    for p in range(src_out.shape[0]):
        src_out[p] = mine
    tgt_out[...] = jnp.concatenate([ref[...] for ref in here[3:]], axis=1)


def prepare_kernel(
    tgt, src_logit_in, tgt_logit_in, src_weight_in, tgt_weight_in,
    xt, right, src_rows, tgt_logit, src_weight, tgt_weight, sums, src_logit, sem,
):
    copies = fetch(
        (src_logit_in, tgt_logit_in, src_weight_in, tgt_weight_in),
        (src_logit, tgt_logit, src_weight, tgt_weight),
        sem,
    )
    rank = tgt.shape[0]
    m = tgt_logit.shape[1]
    xt[:rank] = tgt[:, :m]
    right[:rank] = tgt[:, 2 * m :]
    right[rank : 2 * rank] = tgt[:, 2 * m :]
    row = lax.broadcasted_iota(jnp.int32, (PAD, m), 0)
    right[2 * rank :] = jnp.where(row == 0, 1.0, 0.0).astype(BF16)
    for copy in copies:
        copy.wait()
    src_rows[...] = logit_rows(src_logit[...], True)
    xt[rank:] = logit_rows(tgt_logit[...], False)
    src_sum = jnp.sum(src_weight[...], keepdims=True)
    tgt_sum = jnp.sum(tgt_weight[...], keepdims=True)
    lane = lax.broadcasted_iota(jnp.int32, (1, LANES), 1)
    sums[...] = jnp.where(lane == 1, src_sum, jnp.where(lane == 2, tgt_sum, 0.0))


def opening_kernel(src, xt, right, src_rows, known, out, xs, flat):
    rank = src.shape[0]
    n = src_rows.shape[1]
    xs[:rank] = (src[:, :n].astype(F32) * 0.125).astype(BF16)
    xs[rank:] = src_rows[...]
    row = lax.broadcasted_iota(jnp.int32, (PAD, n), 0)
    left = jnp.concatenate([src[:, 2 * n :], jnp.where(row == 0, 1.0, 0.0).astype(BF16)], axis=0)
    tile = jnp.exp(dot(xs[...], xt[...], FIRST)).astype(BF16)
    side = dot(left, tile, PLAIN)
    both = in_parts(side, right[...])
    core = halves_on_lanes(both[:, : 2 * rank], rank)
    total = both[rank : rank + 1, 2 * rank : 2 * rank + 1]
    lane = lax.broadcasted_iota(jnp.int32, (1, LANES), 1)
    sums = jnp.where(lane == 0, total, known[...])
    parts, _, width = flat.shape
    for q in range(parts):
        for s in range(width // LANES - 1):
            k = q * (width // LANES - 1) + s
            flat[q, :, s * LANES : (s + 1) * LANES] = core[k : k + 1]
        flat[q, :, width - LANES :] = sums
    for p in range(out.shape[0]):
        out[p] = flat[p % parts]


def relay_kernel(y, out):
    send(out, received(y))


def tile_kernel(
    mass_scale, row_peers, col_peers,
    z, src, tgt, src_rows, tgt_logit, src_weight, tgt_weight,
    kernel, flipped, out, row_mass, col_mass,
    xs, xt, totals, tiles, core,
):
    rank = src.shape[0]
    half = rank // 2
    n = src_rows.shape[1]
    m = tgt_logit.shape[1]
    parts, _, width = z.shape
    for q in range(parts):
        for s in range(width // LANES - 1):
            k = q * (width // LANES - 1) + s
            core[k : k + 1] = z[q, :, s * LANES : (s + 1) * LANES]
    sums = z[0, :, width - LANES :]
    grand_total = sums[:, 0:1]
    mixing = mass_scale * core[...] / grand_total
    parts = jnp.concatenate(three_parts(mixing), axis=0).astype(BF16)
    top = src[:half, n : 2 * n]
    bottom = src[half:, n : 2 * n]
    top = dot(parts, jnp.concatenate([top, top, top], axis=0), FIRST)
    bottom = dot(parts, jnp.concatenate([bottom, bottom, bottom], axis=0), FIRST)
    xs[:rank] = (src[:, :n].astype(F32) * 0.125).astype(BF16)
    xs[rank : 2 * rank] = (2.0 * (top[:rank] + bottom[rank:])).astype(BF16)
    row_mass[...] = src_weight[...] / (sums[:, 1:2] / col_peers)
    col_mass[...] = tgt_weight[...] / (sums[:, 2:3] / row_peers)
    xs[2 * rank :] = src_rows[...]
    xt[:rank] = tgt[:, :m]
    xt[rank : 2 * rank] = tgt[:, m : 2 * m]
    xt[2 * rank :] = logit_rows(tgt_logit[...] - jnp.log(grand_total), False)
    tile = jnp.exp(dot(xs[...], xt[...], FIRST)).astype(BF16)
    kernel[...] = tile
    turned = tile.T
    flipped[...] = turned
    totals[...] = dot(jnp.ones((8, m), BF16), turned, PLAIN)
    send(out, to_tiles(totals[0:1], tiles))


def sweep_kernel(y, mass, kernel, out, *rest):
    *scale, flat, tiles = rest
    s = mass[...] / received(y)
    for ref in scale:
        ref[...] = s
    weights = to_lanes(s, flat).astype(BF16)
    send(out, to_tiles(dot(weights, kernel[...], PLAIN)[0:1], tiles))


def side_kernel(shift, row_scale, src, kernel, row_potential, side, flat, tile, sem):
    rank = src.shape[0]
    slabs, rows, _ = tile.shape
    n = slabs * rows
    copies = fetch(
        [kernel.at[pl.ds(k * rows, rows)] for k in range(slabs)],
        [tile.at[k] for k in range(slabs)],
        sem,
    )
    row_potential[...] = jnp.log(row_scale[...]) + shift
    scale = to_lanes(row_scale[...], flat)
    left = src[:, 2 * n :].astype(F32) * scale[0:1]
    parts = jnp.concatenate(three_parts(left), axis=0).astype(BF16)
    total = 0.0
    for k, copy in enumerate(copies):
        copy.wait()
        total = total + dot(parts[:, k * rows : (k + 1) * rows], tile[k], PLAIN)
    side[...] = total[:rank] + total[rank : 2 * rank] + total[2 * rank :]


def closing_kernel(y, mass, side, tgt, col_potential, out, flat, twice, potential, sem):
    rank, m = side.shape
    col_scale = mass[...] / received(y)
    potential[...] = jnp.log(col_scale)
    (copy,) = fetch([potential], [col_potential], sem)
    cols = to_lanes(col_scale, flat)
    scaled = (tgt[:, 2 * m :].astype(F32) * cols[0:1]).astype(BF16)
    twice[:rank] = scaled
    twice[rank:] = scaled
    send(out, halves_on_lanes(in_parts(side[...], twice[...]), rank))
    copy.wait()


def final_kernel(mass_scale, y, out):
    core = mass_scale * received(y)
    half, rank = core.shape[0], core.shape[1] // 2
    out[:half] = core[:, :rank]
    out[half:] = core[:, rank:]


def call(body, outs, scratch, *args, stay=0, out_stay=0, room=8):
    here, there = args[: len(args) - stay], args[len(args) - stay :]
    there = [pltpu.with_memory_space_constraint(a, pltpu.HBM) for a in there]
    return pl.pallas_call(
        body,
        out_shape=[jax.ShapeDtypeStruct(s, d) for s, d in outs],
        in_specs=[VMEM] * (len(args) - stay) + [HBM] * stay,
        out_specs=[HBM] * out_stay + [VMEM] * (len(outs) - out_stay),
        scratch_shapes=[pltpu.VMEM(*x) if isinstance(x, tuple) else x for x in scratch],
        compiler_params=pltpu.CompilerParams(vmem_limit_bytes=room << 20),
    )(*here, *there)


def exchange(value, axis):
    return lax.all_to_all(value, axis, 0, 0, tiled=True)


def body(
    src_embed,
    src_left,
    src_right,
    src_logit,
    src_weight,
    tgt_embed,
    tgt_left,
    tgt_right,
    tgt_logit,
    tgt_weight,
):
    n, m = src_logit.shape[0], tgt_logit.shape[0]
    row_peers, col_peers = lax.axis_size(ROW), lax.axis_size(COL)
    n_all, m_all = n * row_peers, m * col_peers
    rank = src_embed.shape[0] * col_peers
    half = rank // 2
    mass_scale = math.sqrt(n_all * m_all)
    nt, mt = n // LANES, m // LANES

    src, tgt = call(
        pack_kernel,
        [
            ((col_peers, rank // col_peers, 3 * n), BF16),
            ((rank // row_peers, 3 * m), BF16),
        ],
        [
            *[(a.shape, BF16) for a in (src_embed, src_left, src_right)],
            *[(a.shape, BF16) for a in (tgt_embed, tgt_left, tgt_right)],
            pltpu.SemaphoreType.DMA((6,)),
        ],
        src_embed, src_left, src_right, tgt_embed, tgt_left, tgt_right, stay=6,
    )
    src = exchange(src, COL).reshape(rank, 3 * n)
    tgt = lax.all_gather(tgt, ROW, axis=0, tiled=True)
    src_logit, tgt_logit = src_logit.reshape(1, n), tgt_logit.reshape(1, m)
    src_weight, tgt_weight = src_weight.reshape(nt, LANES), tgt_weight.reshape(mt, LANES)

    near = lax.axis_size(NEAR)
    width = half * LANES // near + LANES
    xt, right, src_rows, tgt_logit, src_weight, tgt_weight, known = call(
        prepare_kernel,
        [
            ((rank + PAD, m), BF16),
            ((2 * rank + PAD, m), BF16),
            ((PAD, n), BF16),
            ((1, m), F32),
            ((nt, LANES), F32),
            ((mt, LANES), F32),
            ((1, LANES), F32),
        ],
        [((1, n), F32), pltpu.SemaphoreType.DMA((4,))],
        tgt, src_logit, tgt_logit, src_weight, tgt_weight, stay=4,
    )
    (part,) = call(
        opening_kernel,
        [((row_peers, 1, width), F32)],
        [((rank + PAD, n), BF16), ((near, 1, width), F32)],
        src, xt, right, src_rows, known, room=32,
    )
    (part,) = call(relay_kernel, [((col_peers, 1, width), F32)], [], exchange(part, ROW))
    (part,) = call(relay_kernel, [((near, 1, width), F32)], [], exchange(part, COL))
    kernel, flipped, part, row_mass, col_mass = call(
        functools.partial(tile_kernel, mass_scale, row_peers, col_peers),
        [
            ((n, m), BF16),
            ((m, n), BF16),
            ((col_peers, nt, LANES), BF16),
            ((nt, LANES), F32),
            ((mt, LANES), F32),
        ],
        [
            ((2 * rank + PAD, n), BF16),
            ((2 * rank + PAD, m), BF16),
            ((8, n), F32),
            ((nt, LANES), F32),
            ((half, LANES), F32),
        ],
        exchange(part, NEAR), src, tgt, src_rows, tgt_logit, src_weight, tgt_weight, room=32,
    )
    for sweep in range(SWEEPS):
        last = sweep + 1 == SWEEPS
        part, *row_scale = call(
            sweep_kernel,
            [((row_peers, mt, LANES), BF16), ((nt, LANES), F32)][: 1 + last],
            [((8, n), F32), ((mt, LANES), F32)],
            exchange(part, COL), row_mass, kernel,
        )
        part = exchange(part, ROW)
        if not last:
            (part,) = call(
                sweep_kernel,
                [((col_peers, nt, LANES), BF16)],
                [((8, m), F32), ((nt, LANES), F32)],
                part, col_mass, flipped,
            )
    (row_scale,) = row_scale
    row_potential, side = call(
        functools.partial(side_kernel, math.log(n_all) + math.log(m_all)),
        [((nt, LANES), F32), ((rank, m), F32)],
        [((8, n), F32), ((8, n // 8, m), BF16), pltpu.SemaphoreType.DMA((8,))],
        row_scale, src, kernel, stay=1, room=16,
    )
    col_potential, part = call(
        closing_kernel,
        [((mt, LANES), F32), ((row_peers, half, LANES), BF16)],
        [((8, m), F32), ((2 * rank, m), BF16), ((mt, LANES), F32), pltpu.SemaphoreType.DMA((1,))],
        part, col_mass, side, tgt, out_stay=1,
    )
    (part,) = call(relay_kernel, [((col_peers, half, LANES), BF16)], [], exchange(part, ROW))
    (new_core,) = call(
        functools.partial(final_kernel, mass_scale), [((rank, rank), F32)], [], exchange(part, COL)
    )
    return (row_potential.reshape(n), col_potential.reshape(m), new_core)


def solution(mesh):
    torus = Mesh(mesh.devices.reshape(4, 2, 2, 8, 4), ("row_0", "row_1", "core", "col_0", "col_1"))
    placed = (
        P(COL, ROW),
        P(COL, ROW),
        P(COL, ROW),
        P(ROW),
        P(ROW),
        P(ROW, COL),
        P(ROW, COL),
        P(ROW, COL),
        P(COL),
        P(COL),
    )
    return jax.shard_map(
        body, mesh=torus, in_specs=placed, out_specs=(P(ROW), P(COL), P()), check_vma=False
    )
```
